32 devices in a mesh: grp: 2 (over x), probe: 8 (over z, y), beam: 2 (over core).
Axes of the slice: x: 2, y: 2, z: 4, core: 2. Of those that a mesh axis runs over, the one named last changes fastest.
Arguments:
- smatrix: bfloat16 [8192, 8, 512], P(('grp', 'beam'), 'probe'), parts along dimension 0, may hold values from -0.09375 to 0.09375
- aperture: float32 [4096], P('beam'), may hold values from 0.5 to 1.5
- aberration: float32 [4096], P('beam'), may hold values from -3.140625 to 3.140625
- beam_k: int32 [2, 4096], P(None, 'beam'), may hold values from -32 to 31, as said below
- probe_pos: int32 [2, 2048], P(None, 'probe'), may hold values from 0 to 1023
- patches: bfloat16 [128, 512], P(('grp', 'probe')), parts along dimension 0, may hold values from -6 to 6
- patch_col: int32 [128], P('grp'), parts along dimension 0, may hold values from 0 to 7, never falling along the last dimension, each value on 1 to 32 neighbouring positions
Outputs:
- ionization: float32 [16, 2048], P('grp', ('probe', 'beam')), parts along dimension 0
The draws below stay inside these ranges and needn't reach their ends.
There are 2 independent parts, one for each index of `grp`. The reference program is written for one: setup_inputs(seed, part) draws one part's arguments, and reference() takes and returns one part's arrays. A program takes and returns all parts, laid end to end along the dimension named above; an argument that names none is the same for every part. Nothing has to cross between parts.
Inputs may be any that keep to these rules, and one draw needn't show every extreme that they name: `patch_col`: patches are ordered by atom column; each of the 8 columns has 1 to 32 patches, and some column has exactly 32. `beam_k`: no two beams have the same pair of indices.
All inputs are finite; a program needn't handle non-finite values.
Results may differ from the reference program's by a relative error of at most 0.005.
Values may be sent and summed in bfloat16 or wider, within the bound.
A program may use at most 128 MiB of HBM per device.

```python
import math
import jax
import jax.numpy as jnp
import numpy as np
from jax import lax

NB = 4096
PSIDE = 16
PIX = 256
GRID = 1024
KMAX = 32
NCOL = 8
NPATCH = 64
MOSTP = 32
PTOT = 2048


def draw_beam_k(key, part):
    side_count = 2 * KMAX
    total_points = side_count * side_count
    rank_score = jax.random.permutation(jax.random.fold_in(key, 11), total_points).astype(jnp.int32) + 2
    grid_index = jnp.arange(total_points, dtype=jnp.int32)
    rank_score = jnp.where(grid_index == 0, 0, rank_score)
    rank_score = jnp.where(grid_index == total_points - 1, 1, rank_score)
    chosen_points = jnp.argsort(rank_score, stable=True)[:NB].astype(jnp.int32)
    shuffled = jax.random.permutation(jax.random.fold_in(key, 23), chosen_points).astype(jnp.int32)
    first_index = shuffled // side_count - KMAX
    second_index = shuffled % side_count - KMAX
    return jnp.stack([first_index, second_index]).astype(jnp.int32)


def touch_ends(values, own_key, low, largest):
    place = [jax.random.randint(jax.random.fold_in(own_key, axis), (), 0, length) for axis, length in enumerate(values.shape)]
    main_axis = values.shape.index(max(values.shape))
    neighbour = place[:main_axis] + [(place[main_axis] + 1) % values.shape[main_axis]] + place[main_axis + 1:]
    return values.at[tuple(place)].set(low).at[tuple(neighbour)].set(largest)


def levels(rng, extent, cuts, low, high):
    level, own = 1.0, jax.random.fold_in(rng, 6)
    for position, shards_of in cuts:
        heights = jnp.exp(jax.random.uniform(jax.random.fold_in(own, position), (shards_of,), jnp.float32, low / len(cuts), high / len(cuts)))
        level = level * jnp.repeat(heights, extent[position] // shards_of).reshape([-1 if axis == position else 1 for axis in range(len(extent))])
    return level


def split_up(number_of, total, most, skew):
    weights = [(1 << 20) // math.isqrt(rank ** skew) + 1 for rank in range(2, number_of + 1)]
    spare, counts = total - most - (number_of - 1), [1] * (number_of - 1)
    while spare > 0:
        free = [i for i in range(number_of - 1) if counts[i] < most]
        whole, remaining = sum([weights[i] for i in free]), spare
        for i in free:
            extra = min(most - counts[i], max(1, remaining * weights[i] // whole), spare)
            counts[i] = counts[i] + extra
            spare = spare - extra
    return np.array([most] + counts)


def ragged_sizes(own_key, count, total, limit, skew):
    if count == 2:
        one = jax.random.randint(own_key, (), max(1, total - limit), min(limit, total - 1) + 1)
        return jnp.stack([one, total - one])
    lengths = jnp.asarray(split_up(count, total, limit, skew), jnp.int32)
    pairs = (count - 1) // 2
    giver, receiver = lengths[1:1 + 2 * pairs:2], lengths[2:2 + 2 * pairs:2]
    margin = jnp.minimum(giver - 1, limit - receiver)
    moved = jax.random.randint(jax.random.fold_in(own_key, 1), (pairs,), 0, 1 << 20) % (margin + 1)
    lengths = lengths.at[1:1 + 2 * pairs:2].set(giver - moved).at[2:2 + 2 * pairs:2].set(receiver + moved)
    return lengths[jax.random.permutation(jax.random.fold_in(own_key, 2), count)]


def bell_draw(stream_key, shape, deviation, most, pieces=(), kind=jnp.bfloat16):
    factor_of = levels(stream_key, shape, pieces, -0.22, 0.18) if pieces else 1.0
    values = jax.random.normal(stream_key, shape, jnp.float32) * deviation * factor_of
    return jnp.minimum(jnp.maximum(values, -most), most).astype(kind)


def setup_inputs(seed: int = 0, part: int = 0) -> dict:
    arg_keys = jax.random.split(jax.random.key(seed), 8)
    part_keys = jax.random.split(jax.random.fold_in(arg_keys[7], part), 8)
    smatrix = bell_draw(part_keys[0], (NB, NCOL, 2 * PIX), NB ** -0.5, 0.09375, ((0, 2), (1, 8)))
    aperture = jnp.clip(0.5 + 1.0 * jax.random.uniform(arg_keys[1], (NB,), jnp.float32) ** levels(arg_keys[1], (NB,), ((0, 2),), -0.2, 0.2), 0.5, 1.5)
    aberration = jnp.clip(jax.random.uniform(arg_keys[2], (NB,), jnp.float32, -3.140625, 3.140625), -3.140625, 3.140625)
    beam_k = draw_beam_k(jax.random.fold_in(arg_keys[7], 71), part)
    probe_pos = touch_ends(jax.random.randint(arg_keys[4], (2, PTOT), 0, GRID), jax.random.fold_in(arg_keys[4], 1), 0, GRID - 1).astype(jnp.int32)
    patches = bell_draw(part_keys[5], (NPATCH, 2 * PIX), 1.0, 6.0, ((0, 8),))
    patch_col = jnp.searchsorted(jnp.cumsum(ragged_sizes(part_keys[6], NCOL, NPATCH, MOSTP, 2)), jnp.arange(NPATCH), side="right").astype(jnp.int32)
    return dict(smatrix=smatrix, aperture=aperture, aberration=aberration, beam_k=beam_k, probe_pos=probe_pos, patches=patches, patch_col=patch_col)


def coefficients(beam_k, aperture, aberration, positions):
    turn_count = jnp.mod(positions[0][:, None] * beam_k[0][None, :] + positions[1][:, None] * beam_k[1][None, :], GRID)
    phase_angle = aberration[None, :] + (2.0 * math.pi / GRID) * turn_count.astype(jnp.float32)
    real_coef = (aperture[None, :] * jnp.cos(phase_angle)).astype(jnp.bfloat16)
    imag_coef = (-(aperture[None, :] * jnp.sin(phase_angle))).astype(jnp.bfloat16)
    return real_coef, imag_coef


def detector(edge_count):
    half_side = edge_count // 2
    pixel_index = jnp.arange(edge_count * edge_count, dtype=jnp.int32)
    mode_index = jnp.arange(edge_count * half_side, dtype=jnp.int32)
    row_off = pixel_index // edge_count
    col_off = pixel_index % edge_count
    freq_first = mode_index // half_side - half_side
    freq_second = mode_index % half_side - edge_count // 4
    turn_count = jnp.mod(row_off[:, None] * freq_first[None, :] + col_off[:, None] * freq_second[None, :], edge_count)
    angle_value = (2.0 * math.pi / edge_count) * turn_count.astype(jnp.float32)
    real_part = jnp.cos(angle_value)
    imag_part = -jnp.sin(angle_value)
    upper_rows = jnp.concatenate([real_part, imag_part], axis=1)
    lower_rows = jnp.concatenate([-imag_part, real_part], axis=1)
    return jnp.concatenate([upper_rows, lower_rows], axis=0).astype(jnp.bfloat16)


def patch_energy(picked, pot_rows, det_table):
    half_width = pot_rows.shape[-1] // 2
    psi_re = picked[..., :half_width].astype(jnp.float32)
    psi_im = picked[..., half_width:].astype(jnp.float32)
    pot_re = pot_rows[:, :half_width].astype(jnp.float32)
    pot_im = pot_rows[:, half_width:].astype(jnp.float32)
    wave_out = jnp.concatenate([psi_re * pot_re - psi_im * pot_im, psi_re * pot_im + psi_im * pot_re], axis=-1).astype(jnp.bfloat16)
    projected = jnp.einsum("rjx,xq->rjq", wave_out.astype(jnp.float32), det_table.astype(jnp.float32))
    return jnp.sum(projected * projected, axis=-1) / float(half_width * (det_table.shape[1] // 2))


def reference(smatrix, aperture, aberration, beam_k, probe_pos, patches, patch_col):
    det_table = detector(PSIDE)
    half_width = smatrix.shape[2] // 2
    flat_matrix = smatrix.reshape(NB, NCOL * 2 * half_width)
    block_rows = math.gcd(PTOT, 512)
    pos_blocks = probe_pos.reshape(2, PTOT // block_rows, block_rows).transpose(1, 0, 2)
    onehot = (patch_col[:, None] == jnp.arange(NCOL, dtype=jnp.int32)[None, :]).astype(jnp.float32)

    def per_block(positions):
        real_coef, imag_coef = coefficients(beam_k, aperture, aberration, positions)
        from_re = jnp.dot(real_coef, flat_matrix, preferred_element_type=jnp.float32).reshape(block_rows, NCOL, 2 * half_width)
        from_im = jnp.dot(imag_coef, flat_matrix, preferred_element_type=jnp.float32).reshape(block_rows, NCOL, 2 * half_width)
        psi = jnp.concatenate([from_re[..., :half_width] - from_im[..., half_width:], from_re[..., half_width:] + from_im[..., :half_width]], axis=-1).astype(jnp.bfloat16)
        picked = jnp.take(psi, patch_col, axis=1)
        energy = patch_energy(picked, patches, det_table)
        return jnp.dot(energy, onehot, precision=lax.Precision.HIGHEST)

    result = lax.map(per_block, pos_blocks)
    return result.reshape(PTOT, NCOL).T
```

```python
import math

import jax
import jax.numpy as jnp
from jax import lax
from jax.sharding import PartitionSpec as P

PSIDE = 16
GRID = 1024


def coefficients(beam_k, beam_cos, beam_sin, positions):
    turn_count = (
        positions[0][:, None] * beam_k[0][None, :] + positions[1][:, None] * beam_k[1][None, :]
    ) & (GRID - 1)
    quarter = GRID // 4
    quadrant = lax.shift_right_arithmetic(turn_count + quarter // 2, quarter.bit_length() - 1)
    resid = (turn_count - quadrant * quarter).astype(jnp.float32) * (2.0 * math.pi / GRID)
    sq = resid * resid
    sin_r = resid + resid * sq * (
        -1.0 / 6 + sq * (1.0 / 120 + sq * (-1.0 / 5040 + sq * (1.0 / 362880)))
    )
    cos_r = 1.0 + sq * (-0.5 + sq * (1.0 / 24 + sq * (-1.0 / 720 + sq * (1.0 / 40320))))
    odd = (quadrant & 1) == 1
    cos_mag = jnp.where(odd, sin_r, cos_r)
    sin_mag = jnp.where(odd, cos_r, sin_r)
    cos_t = jnp.where(((quadrant + 1) & 2) != 0, -cos_mag, cos_mag)
    sin_t = jnp.where((quadrant & 2) != 0, -sin_mag, sin_mag)
    real_coef = (beam_cos[None, :] * cos_t - beam_sin[None, :] * sin_t).astype(jnp.bfloat16)
    imag_coef = (-(beam_sin[None, :] * cos_t + beam_cos[None, :] * sin_t)).astype(jnp.bfloat16)
    return (real_coef, imag_coef)


def detector(edge_count):
    half_side = edge_count // 2
    pixel_index = jnp.arange(edge_count * edge_count, dtype=jnp.int32)
    mode_index = jnp.arange(edge_count * half_side, dtype=jnp.int32)
    row_off = pixel_index // edge_count
    col_off = pixel_index % edge_count
    freq_first = mode_index // half_side - half_side
    freq_second = mode_index % half_side - edge_count // 4
    turn_count = jnp.mod(
        row_off[:, None] * freq_first[None, :] + col_off[:, None] * freq_second[None, :], edge_count
    )
    angle_value = 2.0 * math.pi / edge_count * turn_count.astype(jnp.float32)
    real_part = jnp.cos(angle_value)
    imag_part = -jnp.sin(angle_value)
    upper_rows = jnp.concatenate([real_part, imag_part], axis=1)
    lower_rows = jnp.concatenate([-imag_part, real_part], axis=1)
    return jnp.concatenate([upper_rows, lower_rows], axis=0).astype(jnp.bfloat16)


def patch_energy(picked, pot_rows, det_table):
    half_width = pot_rows.shape[-1] // 2
    psi_re = picked[..., :half_width].astype(jnp.float32)
    psi_im = picked[..., half_width:].astype(jnp.float32)
    pot_re = pot_rows[:, :half_width].astype(jnp.float32)
    pot_im = pot_rows[:, half_width:].astype(jnp.float32)
    wave_out = jnp.concatenate(
        [psi_re * pot_re - psi_im * pot_im, psi_re * pot_im + psi_im * pot_re], axis=-1
    ).astype(jnp.bfloat16)
    projected = jnp.einsum("rjx,xq->rjq", wave_out, det_table, preferred_element_type=jnp.float32)
    return jnp.sum(projected * projected, axis=-1) / float(half_width * (det_table.shape[1] // 2))


def combine(beam_terms):
    half_width = beam_terms.shape[-1] // 2
    return jnp.concatenate(
        [
            beam_terms[0, ..., :half_width] - beam_terms[1, ..., half_width:],
            beam_terms[0, ..., half_width:] + beam_terms[1, ..., :half_width],
        ],
        axis=-1,
    )


def spread_patches(psi, all_patches, patch_col, det_table):
    patch_total = all_patches.shape[0]
    group_size = math.gcd(patch_total, 16)
    column_count = psi.shape[1]
    col_groups = patch_col.reshape(patch_total // group_size, group_size)
    pot_groups = all_patches.reshape(patch_total // group_size, group_size, all_patches.shape[1])
    col_range = jnp.arange(column_count, dtype=jnp.int32)

    def add_block(running, blk_pair):
        col_ids, pot_rows = blk_pair
        picked = jnp.take(psi, col_ids, axis=1)
        energy = patch_energy(picked, pot_rows, det_table)
        onehot = (col_ids[:, None] == col_range[None, :]).astype(jnp.float32)
        return (
            running + jnp.einsum("rj,jc->cr", energy, onehot, precision=lax.Precision.HIGHEST),
            None,
        )

    running, _ = lax.scan(
        add_block, jnp.zeros((column_count, psi.shape[0]), jnp.float32), (col_groups, pot_groups)
    )
    return running


def apply_patches(psi_own, all_patches, patch_col, det_table):
    traded = lax.all_to_all(psi_own, "probe", split_axis=0, concat_axis=2, tiled=True)
    return spread_patches(traded[0], all_patches, patch_col, det_table)


def shards(smatrix, aperture, aberration, beam_k, probe_pos, patches, patch_col):
    probe_count = lax.axis_size("probe")
    beam_count = lax.axis_size("beam")
    all_patches = lax.all_gather(patches, "probe", axis=0, tiled=True)
    det_table = detector(PSIDE)
    col_dev = smatrix.shape[1]
    width_two = smatrix.shape[2]
    full_matrix = lax.all_gather(smatrix, "beam", axis=0, tiled=True)
    full_cos = lax.all_gather(aperture * jnp.cos(aberration), "beam", axis=0, tiled=True)
    full_sin = lax.all_gather(aperture * jnp.sin(aberration), "beam", axis=0, tiled=True)
    full_k = lax.all_gather(beam_k, "beam", axis=1, tiled=True)
    all_pos = lax.all_gather(probe_pos, "probe", axis=1, tiled=True)
    probe_total = all_pos.shape[1]
    half_probes = probe_total // (beam_count * probe_count)
    split_pos = all_pos.reshape(2, probe_count, beam_count, half_probes)
    mine = lax.dynamic_slice_in_dim(split_pos, lax.axis_index("beam"), 1, 2).reshape(
        2, probe_count * half_probes
    )
    row_total = probe_count * half_probes
    block_rows = math.gcd(row_total, 512)
    pos_blocks = mine.reshape(2, row_total // block_rows, block_rows).transpose(1, 0, 2)

    def whole_block(positions):
        real_coef, imag_coef = coefficients(full_k, full_cos, full_sin, positions)
        beam_terms = jnp.einsum(
            "kpb,bcx->kpcx",
            jnp.stack([real_coef, imag_coef]),
            full_matrix,
            preferred_element_type=jnp.float32,
        )
        return combine(beam_terms).astype(jnp.bfloat16)

    psi_own = lax.map(whole_block, pos_blocks).reshape(probe_count, half_probes, col_dev, width_two)
    return apply_patches(psi_own, all_patches, patch_col, det_table)


def solution(mesh):
    placed = (
        P(("grp", "beam"), "probe", None),
        P("beam"),
        P("beam"),
        P(None, "beam"),
        P(None, "probe"),
        P(("grp", "probe"), None),
        P("grp"),
    )
    return jax.shard_map(
        shards, mesh=mesh, in_specs=placed, out_specs=P("grp", ("probe", "beam")), check_vma=False
    )
```

```python
import math

import jax
import jax.numpy as jnp
from jax import lax
from jax.sharding import PartitionSpec as P

PSIDE = 16
GRID = 1024


def coefficients(beam_k, beam_cos, beam_sin, positions):
    turn_count = (
        positions[0][:, None] * beam_k[0][None, :] + positions[1][:, None] * beam_k[1][None, :]
    ) & (GRID - 1)
    quarter = GRID // 4
    quadrant = lax.shift_right_arithmetic(turn_count + quarter // 2, quarter.bit_length() - 1)
    resid = (turn_count - quadrant * quarter).astype(jnp.float32) * (2.0 * math.pi / GRID)
    sq = resid * resid
    sin_r = resid + resid * sq * (
        -1.0 / 6 + sq * (1.0 / 120 + sq * (-1.0 / 5040 + sq * (1.0 / 362880)))
    )
    cos_r = 1.0 + sq * (-0.5 + sq * (1.0 / 24 + sq * (-1.0 / 720 + sq * (1.0 / 40320))))
    odd = (quadrant & 1) == 1
    cos_mag = jnp.where(odd, sin_r, cos_r)
    sin_mag = jnp.where(odd, cos_r, sin_r)
    cos_t = jnp.where(((quadrant + 1) & 2) != 0, -cos_mag, cos_mag)
    sin_t = jnp.where((quadrant & 2) != 0, -sin_mag, sin_mag)
    real_coef = (beam_cos[None, :] * cos_t - beam_sin[None, :] * sin_t).astype(jnp.bfloat16)
    imag_coef = (-(beam_sin[None, :] * cos_t + beam_cos[None, :] * sin_t)).astype(jnp.bfloat16)
    return (real_coef, imag_coef)


def detector(edge_count):
    half_side = edge_count // 2
    pixel_index = jnp.arange(edge_count * edge_count, dtype=jnp.int32)
    mode_index = jnp.arange(edge_count * half_side, dtype=jnp.int32)
    row_off = pixel_index // edge_count
    col_off = pixel_index % edge_count
    freq_first = mode_index // half_side - half_side
    freq_second = mode_index % half_side - edge_count // 4
    turn_count = jnp.mod(
        row_off[:, None] * freq_first[None, :] + col_off[:, None] * freq_second[None, :], edge_count
    )
    angle_value = 2.0 * math.pi / edge_count * turn_count.astype(jnp.float32)
    real_part = jnp.cos(angle_value)
    imag_part = -jnp.sin(angle_value)
    upper_rows = jnp.concatenate([real_part, imag_part], axis=1)
    lower_rows = jnp.concatenate([-imag_part, real_part], axis=1)
    return jnp.concatenate([upper_rows, lower_rows], axis=0).astype(jnp.bfloat16)


def patch_energy(picked, pot_rows, det_table):
    half_width = pot_rows.shape[-1] // 2
    psi_re = picked[..., :half_width].astype(jnp.float32)
    psi_im = picked[..., half_width:].astype(jnp.float32)
    pot_re = pot_rows[:, :half_width].astype(jnp.float32)
    pot_im = pot_rows[:, half_width:].astype(jnp.float32)
    wave_out = jnp.concatenate(
        [psi_re * pot_re - psi_im * pot_im, psi_re * pot_im + psi_im * pot_re], axis=-1
    ).astype(jnp.bfloat16)
    projected = jnp.einsum("rjx,xq->rjq", wave_out, det_table, preferred_element_type=jnp.float32)
    return jnp.sum(projected * projected, axis=-1) / float(half_width * (det_table.shape[1] // 2))


def combine(beam_terms):
    half_width = beam_terms.shape[-1] // 2
    return jnp.concatenate(
        [
            beam_terms[0, ..., :half_width] - beam_terms[1, ..., half_width:],
            beam_terms[0, ..., half_width:] + beam_terms[1, ..., :half_width],
        ],
        axis=-1,
    )


def spread_patches(psi, all_patches, patch_col, det_table):
    patch_total = all_patches.shape[0]
    group_size = math.gcd(patch_total, 16)
    column_count = psi.shape[1]
    col_groups = patch_col.reshape(patch_total // group_size, group_size)
    pot_groups = all_patches.reshape(patch_total // group_size, group_size, all_patches.shape[1])
    col_range = jnp.arange(column_count, dtype=jnp.int32)

    def add_block(running, blk_pair):
        col_ids, pot_rows = blk_pair
        picked = jnp.take(psi, col_ids, axis=1)
        energy = patch_energy(picked, pot_rows, det_table)
        onehot = (col_ids[:, None] == col_range[None, :]).astype(jnp.float32)
        return (
            running + jnp.einsum("rj,jc->cr", energy, onehot, precision=lax.Precision.HIGHEST),
            None,
        )

    running, _ = lax.scan(
        add_block, jnp.zeros((column_count, psi.shape[0]), jnp.float32), (col_groups, pot_groups)
    )
    return running


def apply_patches(psi_own, all_patches, patch_col, det_table):
    traded = lax.all_to_all(psi_own, "probe", split_axis=0, concat_axis=2, tiled=True)
    return spread_patches(traded[0], all_patches, patch_col, det_table)


def shards(smatrix, aperture, aberration, beam_k, probe_pos, patches, patch_col):
    probe_count = lax.axis_size("probe")
    beam_count = lax.axis_size("beam")
    all_patches = lax.all_gather(patches, "probe", axis=0, tiled=True)
    det_table = detector(PSIDE)
    col_dev = smatrix.shape[1]
    width_two = smatrix.shape[2]
    full_matrix = lax.all_gather(smatrix, "beam", axis=0, tiled=True)
    full_cos = lax.all_gather(aperture * jnp.cos(aberration), "beam", axis=0, tiled=True)
    full_sin = lax.all_gather(aperture * jnp.sin(aberration), "beam", axis=0, tiled=True)
    full_k = lax.all_gather(beam_k, "beam", axis=1, tiled=True)
    all_pos = lax.all_gather(probe_pos, "probe", axis=1, tiled=True)
    all_pos, all_patches = lax.optimization_barrier((all_pos, all_patches))
    probe_total = all_pos.shape[1]
    half_probes = probe_total // (beam_count * probe_count)
    split_pos = all_pos.reshape(2, probe_count, beam_count, half_probes)
    mine = lax.dynamic_slice_in_dim(split_pos, lax.axis_index("beam"), 1, 2).reshape(
        2, probe_count * half_probes
    )
    real_coef, imag_coef = coefficients(full_k, full_cos, full_sin, mine)
    beam_terms = jnp.einsum(
        "kpb,bcx->kpcx",
        jnp.stack([real_coef, imag_coef]),
        full_matrix,
        preferred_element_type=jnp.float32,
    )
    psi_own = combine(beam_terms).astype(jnp.bfloat16).reshape(
        probe_count, half_probes, col_dev, width_two
    )
    return apply_patches(psi_own, all_patches, patch_col, det_table)


def solution(mesh):
    placed = (
        P(("grp", "beam"), "probe", None),
        P("beam"),
        P("beam"),
        P(None, "beam"),
        P(None, "probe"),
        P(("grp", "probe"), None),
        P("grp"),
    )
    return jax.shard_map(
        shards, mesh=mesh, in_specs=placed, out_specs=P("grp", ("probe", "beam")), check_vma=False
    )
```

```python
import math

import jax
import jax.numpy as jnp
from jax import lax
from jax.sharding import PartitionSpec as P

PSIDE = 16
GRID = 1024


def coefficients(beam_k, beam_cos, beam_sin, positions):
    turn_count = (
        positions[0][:, None] * beam_k[0][None, :] + positions[1][:, None] * beam_k[1][None, :]
    ) & (GRID - 1)
    quarter = GRID // 4
    quadrant = lax.shift_right_arithmetic(turn_count + quarter // 2, quarter.bit_length() - 1)
    resid = (turn_count - quadrant * quarter).astype(jnp.float32) * (2.0 * math.pi / GRID)
    sq = resid * resid
    sin_r = resid + resid * sq * (
        -1.0 / 6 + sq * (1.0 / 120 + sq * (-1.0 / 5040 + sq * (1.0 / 362880)))
    )
    cos_r = 1.0 + sq * (-0.5 + sq * (1.0 / 24 + sq * (-1.0 / 720 + sq * (1.0 / 40320))))
    odd = (quadrant & 1) == 1
    cos_mag = jnp.where(odd, sin_r, cos_r)
    sin_mag = jnp.where(odd, cos_r, sin_r)
    cos_t = jnp.where(((quadrant + 1) & 2) != 0, -cos_mag, cos_mag)
    sin_t = jnp.where((quadrant & 2) != 0, -sin_mag, sin_mag)
    real_coef = (beam_cos[None, :] * cos_t - beam_sin[None, :] * sin_t).astype(jnp.bfloat16)
    imag_coef = (-(beam_sin[None, :] * cos_t + beam_cos[None, :] * sin_t)).astype(jnp.bfloat16)
    return (real_coef, imag_coef)


def detector(edge_count):
    half_side = edge_count // 2
    pixel_index = jnp.arange(edge_count * edge_count, dtype=jnp.int32)
    mode_index = jnp.arange(edge_count * half_side, dtype=jnp.int32)
    row_off = pixel_index // edge_count
    col_off = pixel_index % edge_count
    freq_first = mode_index // half_side - half_side
    freq_second = mode_index % half_side - edge_count // 4
    turn_count = jnp.mod(
        row_off[:, None] * freq_first[None, :] + col_off[:, None] * freq_second[None, :], edge_count
    )
    angle_value = 2.0 * math.pi / edge_count * turn_count.astype(jnp.float32)
    real_part = jnp.cos(angle_value)
    imag_part = -jnp.sin(angle_value)
    upper_rows = jnp.concatenate([real_part, imag_part], axis=1)
    lower_rows = jnp.concatenate([-imag_part, real_part], axis=1)
    return jnp.concatenate([upper_rows, lower_rows], axis=0).astype(jnp.bfloat16)


def patch_energy(picked, pot_rows, det_table):
    half_width = pot_rows.shape[-1] // 2
    psi_re = picked[..., :half_width].astype(jnp.float32)
    psi_im = picked[..., half_width:].astype(jnp.float32)
    pot_re = pot_rows[:, :half_width].astype(jnp.float32)
    pot_im = pot_rows[:, half_width:].astype(jnp.float32)
    wave_out = jnp.concatenate(
        [psi_re * pot_re - psi_im * pot_im, psi_re * pot_im + psi_im * pot_re], axis=-1
    ).astype(jnp.bfloat16)
    projected = jnp.einsum("rjx,xq->rjq", wave_out, det_table, preferred_element_type=jnp.float32)
    return jnp.sum(projected * projected, axis=-1) / float(half_width * (det_table.shape[1] // 2))


def combine(beam_terms):
    half_width = beam_terms.shape[-1] // 2
    return jnp.concatenate(
        [
            beam_terms[0, ..., :half_width] - beam_terms[1, ..., half_width:],
            beam_terms[0, ..., half_width:] + beam_terms[1, ..., :half_width],
        ],
        axis=-1,
    )


def spread_patches(psi, all_patches, patch_col, det_table):
    patch_total = all_patches.shape[0]
    group_size = math.gcd(patch_total, 16)
    column_count = psi.shape[1]
    col_groups = patch_col.reshape(patch_total // group_size, group_size)
    pot_groups = all_patches.reshape(patch_total // group_size, group_size, all_patches.shape[1])
    col_range = jnp.arange(column_count, dtype=jnp.int32)

    def add_block(running, blk_pair):
        col_ids, pot_rows = blk_pair
        picked = jnp.take(psi, col_ids, axis=1)
        energy = patch_energy(picked, pot_rows, det_table)
        onehot = (col_ids[:, None] == col_range[None, :]).astype(jnp.float32)
        return (
            running + jnp.einsum("rj,jc->cr", energy, onehot, precision=lax.Precision.HIGHEST),
            None,
        )

    running, _ = lax.scan(
        add_block, jnp.zeros((column_count, psi.shape[0]), jnp.float32), (col_groups, pot_groups)
    )
    return running


def apply_patches(psi_own, all_patches, patch_col, det_table):
    traded = lax.all_to_all(psi_own, "probe", split_axis=0, concat_axis=2, tiled=True)
    return spread_patches(traded[0], all_patches, patch_col, det_table)


def shards(smatrix, aperture, aberration, beam_k, probe_pos, patches, patch_col):
    probe_count = lax.axis_size("probe")
    beam_count = lax.axis_size("beam")
    probe_count_all = lax.axis_size("probe")
    patch_size = patches.size
    packed = jnp.concatenate(
        [patches.astype(jnp.float32).reshape(-1), probe_pos.astype(jnp.float32).reshape(-1)]
    )
    gathered = lax.all_gather(packed, "probe", axis=0)
    all_patches = (
        gathered[:, :patch_size]
        .reshape(probe_count_all * patches.shape[0], patches.shape[1])
        .astype(patches.dtype)
    )
    all_pos = (
        gathered[:, patch_size:]
        .reshape(probe_count_all, 2, probe_pos.shape[1])
        .transpose(1, 0, 2)
        .reshape(2, probe_count_all * probe_pos.shape[1])
        .astype(probe_pos.dtype)
    )
    det_table = detector(PSIDE)
    col_dev = smatrix.shape[1]
    width_two = smatrix.shape[2]
    full_matrix = lax.all_gather(smatrix, "beam", axis=0, tiled=True)
    beam_pack = jnp.stack(
        [
            aperture * jnp.cos(aberration),
            aperture * jnp.sin(aberration),
            beam_k[0].astype(jnp.float32),
            beam_k[1].astype(jnp.float32),
        ]
    )
    beam_all = lax.all_gather(beam_pack, "beam", axis=1, tiled=True)
    full_cos, full_sin = beam_all[0], beam_all[1]
    full_k = beam_all[2:].astype(beam_k.dtype)
    probe_total = all_pos.shape[1]
    half_probes = probe_total // (beam_count * probe_count)
    split_pos = all_pos.reshape(2, probe_count, beam_count, half_probes)
    mine = lax.dynamic_slice_in_dim(split_pos, lax.axis_index("beam"), 1, 2).reshape(
        2, probe_count * half_probes
    )
    row_total = probe_count * half_probes
    block_rows = math.gcd(row_total, 512)
    pos_blocks = mine.reshape(2, row_total // block_rows, block_rows).transpose(1, 0, 2)

    def whole_block(positions):
        real_coef, imag_coef = coefficients(full_k, full_cos, full_sin, positions)
        beam_terms = jnp.einsum(
            "kpb,bcx->kpcx",
            jnp.stack([real_coef, imag_coef]),
            full_matrix,
            preferred_element_type=jnp.float32,
        )
        return combine(beam_terms).astype(jnp.bfloat16)

    psi_own = lax.map(whole_block, pos_blocks).reshape(probe_count, half_probes, col_dev, width_two)
    return apply_patches(psi_own, all_patches, patch_col, det_table)


def solution(mesh):
    placed = (
        P(("grp", "beam"), "probe", None),
        P("beam"),
        P("beam"),
        P(None, "beam"),
        P(None, "probe"),
        P(("grp", "probe"), None),
        P("grp"),
    )
    return jax.shard_map(
        shards, mesh=mesh, in_specs=placed, out_specs=P("grp", ("probe", "beam")), check_vma=False
    )
```

```python
import math

import jax
import jax.numpy as jnp
from jax import lax
from jax.sharding import PartitionSpec as P

PSIDE = 16
GRID = 1024


def coefficients(beam_k, beam_cos, beam_sin, positions):
    turn_count = (
        positions[0][:, None] * beam_k[0][None, :] + positions[1][:, None] * beam_k[1][None, :]
    ) & (GRID - 1)
    quarter = GRID // 4
    quadrant = lax.shift_right_arithmetic(turn_count + quarter // 2, quarter.bit_length() - 1)
    resid = (turn_count - quadrant * quarter).astype(jnp.float32) * (2.0 * math.pi / GRID)
    sq = resid * resid
    sin_r = resid + resid * sq * (
        -1.0 / 6 + sq * (1.0 / 120 + sq * (-1.0 / 5040 + sq * (1.0 / 362880)))
    )
    cos_r = 1.0 + sq * (-0.5 + sq * (1.0 / 24 + sq * (-1.0 / 720 + sq * (1.0 / 40320))))
    odd = (quadrant & 1) == 1
    cos_mag = jnp.where(odd, sin_r, cos_r)
    sin_mag = jnp.where(odd, cos_r, sin_r)
    cos_t = jnp.where(((quadrant + 1) & 2) != 0, -cos_mag, cos_mag)
    sin_t = jnp.where((quadrant & 2) != 0, -sin_mag, sin_mag)
    real_coef = (beam_cos[None, :] * cos_t - beam_sin[None, :] * sin_t).astype(jnp.bfloat16)
    imag_coef = (-(beam_sin[None, :] * cos_t + beam_cos[None, :] * sin_t)).astype(jnp.bfloat16)
    return (real_coef, imag_coef)


def detector(edge_count):
    half_side = edge_count // 2
    pixel_index = jnp.arange(edge_count * edge_count, dtype=jnp.int32)
    mode_index = jnp.arange(edge_count * half_side, dtype=jnp.int32)
    row_off = pixel_index // edge_count
    col_off = pixel_index % edge_count
    freq_first = mode_index // half_side - half_side
    freq_second = mode_index % half_side - edge_count // 4
    turn_count = jnp.mod(
        row_off[:, None] * freq_first[None, :] + col_off[:, None] * freq_second[None, :], edge_count
    )
    angle_value = 2.0 * math.pi / edge_count * turn_count.astype(jnp.float32)
    real_part = jnp.cos(angle_value)
    imag_part = -jnp.sin(angle_value)
    upper_rows = jnp.concatenate([real_part, imag_part], axis=1)
    lower_rows = jnp.concatenate([-imag_part, real_part], axis=1)
    return jnp.concatenate([upper_rows, lower_rows], axis=0).astype(jnp.bfloat16)


def patch_energy(picked, pot_rows, det_table):
    half_width = pot_rows.shape[-1] // 2
    psi_re = picked[..., :half_width].astype(jnp.float32)
    psi_im = picked[..., half_width:].astype(jnp.float32)
    pot_re = pot_rows[:, :half_width].astype(jnp.float32)
    pot_im = pot_rows[:, half_width:].astype(jnp.float32)
    wave_out = jnp.concatenate(
        [psi_re * pot_re - psi_im * pot_im, psi_re * pot_im + psi_im * pot_re], axis=-1
    ).astype(jnp.bfloat16)
    projected = jnp.einsum("rjx,xq->rjq", wave_out, det_table, preferred_element_type=jnp.float32)
    return jnp.sum(projected * projected, axis=-1) / float(half_width * (det_table.shape[1] // 2))


def combine(beam_terms):
    half_width = beam_terms.shape[-1] // 2
    return jnp.concatenate(
        [
            beam_terms[0, ..., :half_width] - beam_terms[1, ..., half_width:],
            beam_terms[0, ..., half_width:] + beam_terms[1, ..., :half_width],
        ],
        axis=-1,
    )


def spread_patches(psi, all_patches, patch_col, det_table):
    patch_total = all_patches.shape[0]
    group_size = math.gcd(patch_total, 16)
    column_count = psi.shape[1]
    col_groups = patch_col.reshape(patch_total // group_size, group_size)
    pot_groups = all_patches.reshape(patch_total // group_size, group_size, all_patches.shape[1])
    col_range = jnp.arange(column_count, dtype=jnp.int32)

    def add_block(running, blk_pair):
        col_ids, pot_rows = blk_pair
        picked = jnp.take(psi, col_ids, axis=1)
        energy = patch_energy(picked, pot_rows, det_table)
        onehot = (col_ids[:, None] == col_range[None, :]).astype(jnp.float32)
        return (
            running + jnp.einsum("rj,jc->cr", energy, onehot, precision=lax.Precision.HIGHEST),
            None,
        )

    running, _ = lax.scan(
        add_block,
        jnp.zeros((column_count, psi.shape[0]), jnp.float32),
        (col_groups, pot_groups),
        unroll=True,
    )
    return running


def apply_patches(psi_own, all_patches, patch_col, det_table):
    traded = lax.all_to_all(psi_own, "probe", split_axis=0, concat_axis=2, tiled=True)
    return spread_patches(traded[0], all_patches, patch_col, det_table)


def shards(smatrix, aperture, aberration, beam_k, probe_pos, patches, patch_col):
    probe_count = lax.axis_size("probe")
    beam_count = lax.axis_size("beam")
    probe_count_all = lax.axis_size("probe")
    patch_size = patches.size
    packed = jnp.concatenate(
        [patches.astype(jnp.float32).reshape(-1), probe_pos.astype(jnp.float32).reshape(-1)]
    )
    gathered = lax.all_gather(packed, "probe", axis=0)
    all_patches = (
        gathered[:, :patch_size]
        .reshape(probe_count_all * patches.shape[0], patches.shape[1])
        .astype(patches.dtype)
    )
    all_pos = (
        gathered[:, patch_size:]
        .reshape(probe_count_all, 2, probe_pos.shape[1])
        .transpose(1, 0, 2)
        .reshape(2, probe_count_all * probe_pos.shape[1])
        .astype(probe_pos.dtype)
    )
    det_table = detector(PSIDE)
    col_dev = smatrix.shape[1]
    width_two = smatrix.shape[2]
    full_matrix = lax.all_gather(smatrix, "beam", axis=0, tiled=True)
    beam_pack = jnp.stack(
        [
            aperture * jnp.cos(aberration),
            aperture * jnp.sin(aberration),
            beam_k[0].astype(jnp.float32),
            beam_k[1].astype(jnp.float32),
        ]
    )
    beam_all = lax.all_gather(beam_pack, "beam", axis=1, tiled=True)
    full_cos, full_sin = beam_all[0], beam_all[1]
    full_k = beam_all[2:].astype(beam_k.dtype)
    probe_total = all_pos.shape[1]
    half_probes = probe_total // (beam_count * probe_count)
    split_pos = all_pos.reshape(2, probe_count, beam_count, half_probes)
    mine = lax.dynamic_slice_in_dim(split_pos, lax.axis_index("beam"), 1, 2).reshape(
        2, probe_count * half_probes
    )
    row_total = probe_count * half_probes
    block_rows = math.gcd(row_total, 512)
    pos_blocks = mine.reshape(2, row_total // block_rows, block_rows).transpose(1, 0, 2)

    def whole_block(positions):
        real_coef, imag_coef = coefficients(full_k, full_cos, full_sin, positions)
        beam_terms = jnp.einsum(
            "kpb,bcx->kpcx",
            jnp.stack([real_coef, imag_coef]),
            full_matrix,
            preferred_element_type=jnp.float32,
        )
        return combine(beam_terms).astype(jnp.bfloat16)

    psi_own = lax.map(whole_block, pos_blocks).reshape(probe_count, half_probes, col_dev, width_two)
    return apply_patches(psi_own, all_patches, patch_col, det_table)


def solution(mesh):
    placed = (
        P(("grp", "beam"), "probe", None),
        P("beam"),
        P("beam"),
        P(None, "beam"),
        P(None, "probe"),
        P(("grp", "probe"), None),
        P("grp"),
    )
    return jax.shard_map(
        shards, mesh=mesh, in_specs=placed, out_specs=P("grp", ("probe", "beam")), check_vma=False
    )
```

```python
import math

import jax
import jax.numpy as jnp
from jax import lax
from jax.sharding import PartitionSpec as P

PSIDE = 16
GRID = 1024


def coefficients(beam_k, beam_cos, beam_sin, positions):
    turn_count = (
        positions[0][:, None] * beam_k[0][None, :] + positions[1][:, None] * beam_k[1][None, :]
    ) & (GRID - 1)
    quarter = GRID // 4
    quadrant = lax.shift_right_arithmetic(turn_count + quarter // 2, quarter.bit_length() - 1)
    resid = (turn_count - quadrant * quarter).astype(jnp.float32) * (2.0 * math.pi / GRID)
    sq = resid * resid
    sin_r = resid + resid * sq * (
        -1.0 / 6 + sq * (1.0 / 120 + sq * (-1.0 / 5040 + sq * (1.0 / 362880)))
    )
    cos_r = 1.0 + sq * (-0.5 + sq * (1.0 / 24 + sq * (-1.0 / 720 + sq * (1.0 / 40320))))
    odd = (quadrant & 1) == 1
    cos_mag = jnp.where(odd, sin_r, cos_r)
    sin_mag = jnp.where(odd, cos_r, sin_r)
    cos_t = jnp.where(((quadrant + 1) & 2) != 0, -cos_mag, cos_mag)
    sin_t = jnp.where((quadrant & 2) != 0, -sin_mag, sin_mag)
    real_coef = (beam_cos[None, :] * cos_t - beam_sin[None, :] * sin_t).astype(jnp.bfloat16)
    imag_coef = (-(beam_sin[None, :] * cos_t + beam_cos[None, :] * sin_t)).astype(jnp.bfloat16)
    return (real_coef, imag_coef)


def detector(edge_count):
    half_side = edge_count // 2
    pixel_index = jnp.arange(edge_count * edge_count, dtype=jnp.int32)
    mode_index = jnp.arange(edge_count * half_side, dtype=jnp.int32)
    row_off = pixel_index // edge_count
    col_off = pixel_index % edge_count
    freq_first = mode_index // half_side - half_side
    freq_second = mode_index % half_side - edge_count // 4
    turn_count = jnp.mod(
        row_off[:, None] * freq_first[None, :] + col_off[:, None] * freq_second[None, :], edge_count
    )
    angle_value = 2.0 * math.pi / edge_count * turn_count.astype(jnp.float32)
    real_part = jnp.cos(angle_value)
    imag_part = -jnp.sin(angle_value)
    upper_rows = jnp.concatenate([real_part, imag_part], axis=1)
    lower_rows = jnp.concatenate([-imag_part, real_part], axis=1)
    return jnp.concatenate([upper_rows, lower_rows], axis=0).astype(jnp.bfloat16)


def patch_energy(picked, pot_rows, det_table):
    half_width = pot_rows.shape[-1] // 2
    psi_re = picked[..., :half_width].astype(jnp.float32)
    psi_im = picked[..., half_width:].astype(jnp.float32)
    pot_re = pot_rows[:, :half_width].astype(jnp.float32)
    pot_im = pot_rows[:, half_width:].astype(jnp.float32)
    wave_out = jnp.concatenate(
        [psi_re * pot_re - psi_im * pot_im, psi_re * pot_im + psi_im * pot_re], axis=-1
    ).astype(jnp.bfloat16)
    projected = jnp.einsum("rjx,xq->rjq", wave_out, det_table, preferred_element_type=jnp.float32)
    return jnp.sum(projected * projected, axis=-1) / float(half_width * (det_table.shape[1] // 2))


def combine(beam_terms):
    half_width = beam_terms.shape[-1] // 2
    return jnp.concatenate(
        [
            beam_terms[0, ..., :half_width] - beam_terms[1, ..., half_width:],
            beam_terms[0, ..., half_width:] + beam_terms[1, ..., :half_width],
        ],
        axis=-1,
    )


def spread_patches(psi, all_patches, patch_col, det_table):
    patch_total = all_patches.shape[0]
    group_size = math.gcd(patch_total, 16)
    column_count = psi.shape[1]
    col_groups = patch_col.reshape(patch_total // group_size, group_size)
    pot_groups = all_patches.reshape(patch_total // group_size, group_size, all_patches.shape[1])
    col_range = jnp.arange(column_count, dtype=jnp.int32)

    def add_block(running, blk_pair):
        col_ids, pot_rows = blk_pair
        picked = jnp.take(psi, col_ids, axis=1)
        energy = patch_energy(picked, pot_rows, det_table)
        onehot = (col_ids[:, None] == col_range[None, :]).astype(jnp.float32)
        return (
            running + jnp.einsum("rj,jc->cr", energy, onehot, precision=lax.Precision.HIGHEST),
            None,
        )

    running, _ = lax.scan(
        add_block, jnp.zeros((column_count, psi.shape[0]), jnp.float32), (col_groups, pot_groups)
    )
    return running


def apply_patches(psi_own, all_patches, patch_col, det_table):
    traded = lax.all_to_all(psi_own, "probe", split_axis=0, concat_axis=2, tiled=True)
    return spread_patches(traded[0], all_patches, patch_col, det_table)


def shards(smatrix, aperture, aberration, beam_k, probe_pos, patches, patch_col):
    probe_count = lax.axis_size("probe")
    beam_count = lax.axis_size("beam")
    probe_count_all = lax.axis_size("probe")
    patch_size = patches.size
    packed = jnp.concatenate(
        [patches.astype(jnp.float32).reshape(-1), probe_pos.astype(jnp.float32).reshape(-1)]
    )
    gathered = lax.all_gather(packed, "probe", axis=0)
    all_patches = (
        gathered[:, :patch_size]
        .reshape(probe_count_all * patches.shape[0], patches.shape[1])
        .astype(patches.dtype)
    )
    all_pos = (
        gathered[:, patch_size:]
        .reshape(probe_count_all, 2, probe_pos.shape[1])
        .transpose(1, 0, 2)
        .reshape(2, probe_count_all * probe_pos.shape[1])
        .astype(probe_pos.dtype)
    )
    det_table = detector(PSIDE)
    col_dev = smatrix.shape[1]
    width_two = smatrix.shape[2]
    full_matrix = lax.all_gather(smatrix, "beam", axis=0, tiled=True)
    beam_pack = jnp.stack(
        [
            aperture * jnp.cos(aberration),
            aperture * jnp.sin(aberration),
            beam_k[0].astype(jnp.float32),
            beam_k[1].astype(jnp.float32),
        ]
    )
    beam_all = lax.all_gather(beam_pack, "beam", axis=1, tiled=True)
    full_cos, full_sin = beam_all[0], beam_all[1]
    full_k = beam_all[2:].astype(beam_k.dtype)
    probe_total = all_pos.shape[1]
    half_probes = probe_total // (beam_count * probe_count)
    split_pos = all_pos.reshape(2, probe_count, beam_count, half_probes)
    mine = lax.dynamic_slice_in_dim(split_pos, lax.axis_index("beam"), 1, 2).reshape(
        2, probe_count * half_probes
    )
    halves = 2 if half_probes % 16 == 0 else 1
    part_rows = half_probes // halves
    pos_parts = mine.reshape(2, probe_count, halves, part_rows).transpose(2, 0, 1, 3)

    def whole_block(positions):
        real_coef, imag_coef = coefficients(full_k, full_cos, full_sin, positions)
        beam_terms = jnp.einsum(
            "kpb,bcx->kpcx",
            jnp.stack([real_coef, imag_coef]),
            full_matrix,
            preferred_element_type=jnp.float32,
        )
        return combine(beam_terms).astype(jnp.bfloat16)

    energies = []
    for part in range(halves):
        psi_part = whole_block(pos_parts[part].reshape(2, probe_count * part_rows)).reshape(
            probe_count, part_rows, col_dev, width_two
        )
        energies.append(apply_patches(psi_part, all_patches, patch_col, det_table))
    return jnp.concatenate(energies, axis=1)


def solution(mesh):
    placed = (
        P(("grp", "beam"), "probe", None),
        P("beam"),
        P("beam"),
        P(None, "beam"),
        P(None, "probe"),
        P(("grp", "probe"), None),
        P("grp"),
    )
    return jax.shard_map(
        shards, mesh=mesh, in_specs=placed, out_specs=P("grp", ("probe", "beam")), check_vma=False
    )
```

```python
import math

import jax
import jax.numpy as jnp
from jax import lax
from jax.sharding import PartitionSpec as P

PSIDE = 16
GRID = 1024


def coefficients(beam_k, beam_cos, beam_sin, positions):
    turn_count = (
        positions[0][:, None] * beam_k[0][None, :] + positions[1][:, None] * beam_k[1][None, :]
    ) & (GRID - 1)
    quarter = GRID // 4
    quadrant = lax.shift_right_arithmetic(turn_count + quarter // 2, quarter.bit_length() - 1)
    resid = (turn_count - quadrant * quarter).astype(jnp.float32) * (2.0 * math.pi / GRID)
    sq = resid * resid
    sin_r = resid + resid * sq * (
        -1.0 / 6 + sq * (1.0 / 120 + sq * (-1.0 / 5040 + sq * (1.0 / 362880)))
    )
    cos_r = 1.0 + sq * (-0.5 + sq * (1.0 / 24 + sq * (-1.0 / 720 + sq * (1.0 / 40320))))
    odd = (quadrant & 1) == 1
    cos_mag = jnp.where(odd, sin_r, cos_r)
    sin_mag = jnp.where(odd, cos_r, sin_r)
    cos_t = jnp.where(((quadrant + 1) & 2) != 0, -cos_mag, cos_mag)
    sin_t = jnp.where((quadrant & 2) != 0, -sin_mag, sin_mag)
    real_coef = (beam_cos[None, :] * cos_t - beam_sin[None, :] * sin_t).astype(jnp.bfloat16)
    imag_coef = (-(beam_sin[None, :] * cos_t + beam_cos[None, :] * sin_t)).astype(jnp.bfloat16)
    return (real_coef, imag_coef)


def detector(edge_count):
    half_side = edge_count // 2
    pixel_index = jnp.arange(edge_count * edge_count, dtype=jnp.int32)
    mode_index = jnp.arange(edge_count * half_side, dtype=jnp.int32)
    row_off = pixel_index // edge_count
    col_off = pixel_index % edge_count
    freq_first = mode_index // half_side - half_side
    freq_second = mode_index % half_side - edge_count // 4
    turn_count = jnp.mod(
        row_off[:, None] * freq_first[None, :] + col_off[:, None] * freq_second[None, :], edge_count
    )
    angle_value = 2.0 * math.pi / edge_count * turn_count.astype(jnp.float32)
    real_part = jnp.cos(angle_value)
    imag_part = -jnp.sin(angle_value)
    upper_rows = jnp.concatenate([real_part, imag_part], axis=1)
    lower_rows = jnp.concatenate([-imag_part, real_part], axis=1)
    return jnp.concatenate([upper_rows, lower_rows], axis=0).astype(jnp.bfloat16)


def patch_energy(picked, pot_rows, det_table):
    half_width = pot_rows.shape[-1] // 2
    psi_re = picked[..., :half_width].astype(jnp.float32)
    psi_im = picked[..., half_width:].astype(jnp.float32)
    pot_re = pot_rows[:, :half_width].astype(jnp.float32)
    pot_im = pot_rows[:, half_width:].astype(jnp.float32)
    wave_out = jnp.concatenate(
        [psi_re * pot_re - psi_im * pot_im, psi_re * pot_im + psi_im * pot_re], axis=-1
    ).astype(jnp.bfloat16)
    projected = jnp.einsum("rjx,xq->rjq", wave_out, det_table, preferred_element_type=jnp.float32)
    return jnp.sum(projected * projected, axis=-1) / float(half_width * (det_table.shape[1] // 2))


def combine(beam_terms):
    half_width = beam_terms.shape[-1] // 2
    return jnp.concatenate(
        [
            beam_terms[0, ..., :half_width] - beam_terms[1, ..., half_width:],
            beam_terms[0, ..., half_width:] + beam_terms[1, ..., :half_width],
        ],
        axis=-1,
    )


def spread_patches(psi, all_patches, patch_col, det_table):
    patch_total = all_patches.shape[0]
    group_size = math.gcd(patch_total, 16)
    column_count = psi.shape[1]
    col_groups = patch_col.reshape(patch_total // group_size, group_size)
    pot_groups = all_patches.reshape(patch_total // group_size, group_size, all_patches.shape[1])
    col_range = jnp.arange(column_count, dtype=jnp.int32)

    def add_block(running, blk_pair):
        col_ids, pot_rows = blk_pair
        picked = jnp.take(psi, col_ids, axis=1)
        energy = patch_energy(picked, pot_rows, det_table)
        onehot = (col_ids[:, None] == col_range[None, :]).astype(jnp.float32)
        return (
            running + jnp.einsum("rj,jc->cr", energy, onehot, precision=lax.Precision.HIGHEST),
            None,
        )

    running, _ = lax.scan(
        add_block, jnp.zeros((column_count, psi.shape[0]), jnp.float32), (col_groups, pot_groups)
    )
    return running


def apply_patches(psi_own, all_patches, patch_col, det_table):
    traded = lax.all_to_all(psi_own, "probe", split_axis=0, concat_axis=2, tiled=True)
    return spread_patches(traded[0], all_patches, patch_col, det_table)


def shards(smatrix, aperture, aberration, beam_k, probe_pos, patches, patch_col):
    probe_count = lax.axis_size("probe")
    beam_count = lax.axis_size("beam")
    probe_count_all = lax.axis_size("probe")
    patch_size = patches.size
    packed = jnp.concatenate(
        [patches.astype(jnp.float32).reshape(-1), probe_pos.astype(jnp.float32).reshape(-1)]
    )
    gathered = lax.all_gather(packed, "probe", axis=0)
    all_patches = (
        gathered[:, :patch_size]
        .reshape(probe_count_all * patches.shape[0], patches.shape[1])
        .astype(patches.dtype)
    )
    all_pos = (
        gathered[:, patch_size:]
        .reshape(probe_count_all, 2, probe_pos.shape[1])
        .transpose(1, 0, 2)
        .reshape(2, probe_count_all * probe_pos.shape[1])
        .astype(probe_pos.dtype)
    )
    det_table = detector(PSIDE)
    col_dev = smatrix.shape[1]
    width_two = smatrix.shape[2]
    full_matrix = lax.all_gather(smatrix, "beam", axis=0, tiled=True)
    beam_pack = jnp.stack(
        [
            aperture * jnp.cos(aberration),
            aperture * jnp.sin(aberration),
            beam_k[0].astype(jnp.float32),
            beam_k[1].astype(jnp.float32),
        ]
    )
    beam_all = lax.all_gather(beam_pack, "beam", axis=1, tiled=True)
    full_cos, full_sin = beam_all[0], beam_all[1]
    full_k = beam_all[2:].astype(beam_k.dtype)
    probe_total = all_pos.shape[1]
    half_probes = probe_total // (beam_count * probe_count)
    split_pos = all_pos.reshape(2, probe_count, beam_count, half_probes)
    mine = lax.dynamic_slice_in_dim(split_pos, lax.axis_index("beam"), 1, 2).reshape(
        2, probe_count * half_probes
    )
    halves = 4 if half_probes % 32 == 0 else 1
    part_rows = half_probes // halves
    pos_parts = mine.reshape(2, probe_count, halves, part_rows).transpose(2, 0, 1, 3)

    def whole_block(positions):
        real_coef, imag_coef = coefficients(full_k, full_cos, full_sin, positions)
        beam_terms = jnp.einsum(
            "kpb,bcx->kpcx",
            jnp.stack([real_coef, imag_coef]),
            full_matrix,
            preferred_element_type=jnp.float32,
        )
        return combine(beam_terms).astype(jnp.bfloat16)

    energies = []
    for part in range(halves):
        psi_part = whole_block(pos_parts[part].reshape(2, probe_count * part_rows)).reshape(
            probe_count, part_rows, col_dev, width_two
        )
        energies.append(apply_patches(psi_part, all_patches, patch_col, det_table))
    return jnp.concatenate(energies, axis=1)


def solution(mesh):
    placed = (
        P(("grp", "beam"), "probe", None),
        P("beam"),
        P("beam"),
        P(None, "beam"),
        P(None, "probe"),
        P(("grp", "probe"), None),
        P("grp"),
    )
    return jax.shard_map(
        shards, mesh=mesh, in_specs=placed, out_specs=P("grp", ("probe", "beam")), check_vma=False
    )
```
